256 devices in a mesh: row: 32 (over z_hi, x, core), col: 8 (over z_lo, y).
Axes of the slice: x: 4, y: 4, z: 8 (z_hi: 4, z_lo: 2; z = z_hi * 2 + z_lo), core: 2. Of those that a mesh axis runs over, the one named last changes fastest.
Arguments:
- left_act: bfloat16 [1024, 4096], P('row', 'col'), may hold values from -18 to 18
- right_act: bfloat16 [1024, 4096], P('col', 'row'), may hold values from -18 to 18
- out_weight: bfloat16 [1024, 128], replicated, may hold values from -0.1875 to 0.1875
- out_bias: float32 [128], replicated, may hold values from -1 to 1
- pair_grad: bfloat16 [1024, 1024, 128], P('row', 'col'), may hold values from -13 to 13
Outputs:
- pair_out: bfloat16 [1024, 1024, 128], P('row', 'col')
- left_grad: float32 [1024, 4096], P('row', 'col')
- right_grad: float32 [1024, 4096], P('col', 'row')
- weight_grad: float32 [1024, 128], replicated
- bias_grad: float32 [128], replicated
The draws below stay inside these ranges and needn't reach their ends.
All inputs are finite; a program needn't handle non-finite values.
Results may differ from the reference program's by a relative error of at most 0.005.
Values may be sent and summed in bfloat16 or wider, within the bound.
No kernel may reach another device: no remote copies, remote signals or barrier semaphores. Data moves between devices by JAX's collectives and lax.ppermute only.
A program may use at most 128 MiB of HBM per device.

```python
import jax
import jax.numpy as jnp
from jax import lax

S = 128
C = 32
CZ = 128
TR = 32
CC = 1024
LI = 1024
LJ = 1024


def draw_pair_grad(key, part):
    first, second = jax.random.split(jax.random.fold_in(key, 7), 2)
    base = jnp.clip(jax.random.normal(first, (LI, LJ, CZ), jnp.float32), -3.0, 3.0)
    rising = 3.0 ** (jnp.arange(LI, dtype=jnp.float32) / max(LI - 1, 1))
    noise = jax.random.uniform(second, (LI, 1, 1), jnp.float32, 0.7, 1.4)
    values = base
    return (values * rising[:, None, None] * noise).astype(jnp.bfloat16)


def level_of(stream_key, shape, shards, least, largest):
    def one(dim, shards_of):
        heights = jax.random.uniform(jax.random.fold_in(jax.random.fold_in(stream_key, 6), dim), (shards_of,), jnp.float32, least / len(shards), largest / len(shards))
        return jnp.repeat(jnp.exp(heights), shape[dim] // shards_of).reshape((-1,) + (1,) * (len(shape) - dim - 1))

    loudness = one(*shards[0])
    for cut in shards[1:]:
        loudness = loudness * one(*cut)
    return loudness


def normal_values(own_key, extent, spread, limit, cuts=(), kind=jnp.bfloat16):
    values = spread * jax.random.normal(own_key, extent, jnp.float32)
    if cuts:
        values = values * level_of(own_key, extent, cuts, -0.22, 0.18)
    return jnp.clip(values, -limit, limit).astype(kind)


def setup_inputs(seed: int = 0) -> dict:
    splits = jax.random.split(jax.random.key(seed), 6)
    left_act = normal_values(splits[0], (LI, S * C), 3.0, 18.0, ((0, 32), (1, 8)))
    right_act = normal_values(splits[1], (LJ, S * C), 3.0, 18.0, ((0, 8), (1, 32)))
    out_weight = normal_values(splits[2], (CC, CZ), CC ** -0.5, 0.1875)
    out_bias = jnp.clip(jax.random.uniform(splits[3], (CZ,), jnp.float32, -1.0, 1.0), -1.0, 1.0)
    pair_grad = draw_pair_grad(jax.random.fold_in(splits[5], 71), 0)
    return dict(left_act=left_act, right_act=right_act, out_weight=out_weight, out_bias=out_bias, pair_grad=pair_grad)


def reference(left_act, right_act, out_weight, out_bias, pair_grad):
    factor = 1.0 / S
    right_tiles = right_act.astype(jnp.float32).reshape(LJ, S, C)
    left_blocks = left_act.astype(jnp.float32).reshape(LI // TR, TR, S, C)
    grad_blocks = pair_grad.reshape(LI // TR, TR, LJ, CZ)

    def advance(carry, inputs):
        weight_sum, bias_sum, right_sum = carry
        left_block, grad_block = inputs
        outer = (jnp.einsum('isc,jsd->ijcd', left_block, right_tiles) * factor).astype(jnp.bfloat16).reshape(TR * LJ, C * C)
        pre = jnp.dot(outer, out_weight, preferred_element_type=jnp.float32) + out_bias
        sigmoid_pre = jax.nn.sigmoid(pre)
        pair_block = (pre * sigmoid_pre).astype(jnp.bfloat16)
        slope = sigmoid_pre * (1.0 + pre * (1.0 - sigmoid_pre))
        dpre = (grad_block.reshape(TR * LJ, CZ).astype(jnp.float32) * slope).astype(jnp.bfloat16)
        weight_sum = weight_sum + jnp.dot(outer.T, dpre, preferred_element_type=jnp.float32)
        bias_sum = bias_sum + jnp.sum(dpre.astype(jnp.float32), axis=0)
        douter = jnp.dot(dpre, out_weight.T, preferred_element_type=jnp.float32).astype(jnp.bfloat16)
        douter = lax.optimization_barrier(douter).astype(jnp.float32).reshape(TR, LJ, C, C)
        left_block_grad = jnp.einsum('ijcd,jsd->isc', douter, right_tiles) * factor
        right_sum = right_sum + jnp.einsum('ijcd,isc->jsd', douter, left_block) * factor
        return (weight_sum, bias_sum, right_sum), (pair_block.reshape(TR, LJ, CZ), left_block_grad.reshape(TR, S * C))

    initial = (jnp.zeros((C * C, CZ), jnp.float32), jnp.zeros((CZ,), jnp.float32), jnp.zeros((LJ, S, C), jnp.float32))
    carry, outputs = lax.scan(advance, initial, (left_blocks, grad_blocks))
    weight_sum, bias_sum, right_sum = carry
    pair_blocks, left_rows = outputs
    return (pair_blocks.reshape(LI, LJ, CZ), left_rows.reshape(LI, S * C), right_sum.reshape(LJ, S * C), weight_sum / LI, bias_sum / LI)
```

```python
import jax
import jax.numpy as jnp
from jax import lax
from jax.experimental import pallas as pl
from jax.experimental.pallas import tpu as pltpu
from jax.sharding import Mesh, PartitionSpec as P

S = 128
C = 32
CZ = 128
CC = C * C
TI = 32
TJ = 128
BF = jnp.bfloat16
F32 = jnp.float32
AXES = ("h", "x", "c", "l", "y")
ROW = ("h", "x", "c")
CHIP = ("h", "x")
COL = ("l", "y")
COST = pl.CostEstimate(flops=6 << 30, transcendentals=0, bytes_accessed=4 << 20)
NN = (((1,), (0,)), ((), ()))
NT = (((1,), (1,)), ((), ()))


def forward_kernel(
    pos_ref, a_ref, mine_ref, other_ref, wt_ref, bias_ref, g_ref,
    po_out, dp_out, b_out, wg_ref,
    at, rows, x, wsum, po_ref, dp_ref, b_ref, sems,
):
    first = pos_ref[2] == 0
    for k in range(4):
        for m in range(4):
            t = ((pos_ref[0] + 4 - m) % 4) * 4 + (pos_ref[1] + 4 - k) % 4
            u = mine_ref[k, m].astype(F32)
            v = other_ref[k, m].astype(F32)
            rows[pl.ds(pl.multiple_of(t * 8, 8), 8), :] = jnp.concatenate(
                [jnp.where(first, u, v), jnp.where(first, v, u)], axis=0
            )
    b_ref[...] = rows[...].astype(BF)
    b_copy = pltpu.make_async_copy(b_ref, b_out, sems.at[0])
    b_copy.start()
    at[...] = a_ref[...].astype(F32).T.astype(BF)
    for n in range(C // 2):
        o = lax.dot_general(
            at[...], b_ref[:, n * 256 : (n + 1) * 256], NN, preferred_element_type=F32
        ).astype(BF)
        for e in range(2):
            d = 2 * n + e
            for i in range(TI):
                x[d * C : (d + 1) * C, i * TJ : (i + 1) * TJ] = o[
                    i * C : (i + 1) * C, e * TJ : (e + 1) * TJ
                ]
    bias = bias_ref[...]
    total = jnp.zeros((8, CZ), F32)
    for q in range(8):
        pre_t = lax.dot_general(
            wt_ref[...], x[:, q * 512 : (q + 1) * 512], NN, preferred_element_type=F32
        )
        pre = pre_t.T + bias
        sig = 1.0 / (1.0 + jnp.exp(-pre))
        po_ref[q * 512 : (q + 1) * 512, :] = (pre * sig).astype(BF)
        slope = sig * (1.0 + pre * (1.0 - sig))
        dpre = (g_ref[q * 512 : (q + 1) * 512, :].astype(F32) * slope).astype(BF)
        dp_ref[q * 512 : (q + 1) * 512, :] = dpre
        total = total + jnp.sum(dpre.astype(F32).reshape(64, 8, CZ), axis=0)
    dp_copy = pltpu.make_async_copy(dp_ref, dp_out, sems.at[1])
    dp_copy.start()
    po_copy = pltpu.make_async_copy(po_ref, po_out, sems.at[2])
    po_copy.start()
    for m in range(4):
        w = lax.dot_general(
            x[m * 256 : (m + 1) * 256, :], dp_ref[...], NN, preferred_element_type=F32
        )
        for k in range(8):
            wsum[pl.ds(m * 8 + k, C, stride=C), :] = w[k * C : (k + 1) * C, :]
    row = jnp.broadcast_to(jnp.sum(total, axis=0, keepdims=True), (8, CZ))
    for c in range(C):
        wg_ref[c, :, :] = jnp.concatenate([wsum[c * C : (c + 1) * C, :], row], axis=0).astype(BF)
    b_copy.wait()
    dp_copy.wait()
    po_copy.wait()


def backward_kernel(
    pos_ref, dp_in, b_in, w_ref, a_ref, rm_ref, ro_ref, l_ref, dd, dp_ref, b_ref, sems
):
    first = pos_ref[2] == 0
    dp_copy = pltpu.make_async_copy(dp_in, dp_ref, sems.at[0])
    dp_copy.start()
    b_copy = pltpu.make_async_copy(b_in, b_ref, sems.at[1])
    b_copy.start()
    dp_copy.wait()
    for q in range(TI // 2):
        g = lax.dot_general(
            w_ref[...], dp_ref[q * 256 : (q + 1) * 256, :], NT, preferred_element_type=F32
        ).astype(BF)
        for e in range(2):
            i = 2 * q + e
            for d in range(C):
                dd[i * C : (i + 1) * C, d * TJ : (d + 1) * TJ] = g[
                    d * C : (d + 1) * C, e * TJ : (e + 1) * TJ
                ]
    for n in range(8):
        r = lax.dot_general(
            a_ref[...], dd[:, n * 512 : (n + 1) * 512], NN, preferred_element_type=F32
        )
        for t in range(16):
            k = (t % 4 + 4 - pos_ref[1]) % 4
            m = (t // 4 + 4 - pos_ref[0]) % 4
            u = r[8 * t : 8 * t + 4, :]
            v = r[8 * t + 4 : 8 * t + 8, :]
            rm_ref[k, m, :, n * 512 : (n + 1) * 512] = jnp.where(first, u, v)
            ro_ref[k, m, :, n * 512 : (n + 1) * 512] = jnp.where(first, v, u).astype(BF)
    b_copy.wait()
    for m in range(4):
        t = lax.dot_general(
            dd[m * 256 : (m + 1) * 256, :], b_ref[...], NT, preferred_element_type=F32
        )
        l_ref[:, m * 256 : (m + 1) * 256] = (t.T * (1.0 / S)).astype(BF)


SCALARS = pl.BlockSpec(memory_space=pltpu.SMEM)
FAR = pl.BlockSpec(memory_space=pltpu.HBM)
WHOLE = pl.BlockSpec(memory_space=pltpu.VMEM)


def forward_call(*args):
    return pl.pallas_call(
        forward_kernel,
        in_specs=[SCALARS] + [WHOLE] * 6,
        out_specs=(FAR, FAR, FAR, WHOLE),
        out_shape=(
            jax.ShapeDtypeStruct((TI * TJ, CZ), BF),
            jax.ShapeDtypeStruct((TI * TJ, CZ), BF),
            jax.ShapeDtypeStruct((S, C * TJ), BF),
            jax.ShapeDtypeStruct((C, C + 8, CZ), BF),
        ),
        scratch_shapes=[
            pltpu.VMEM((TI * C, S), BF),
            pltpu.VMEM((S, C * TJ), F32),
            pltpu.VMEM((CC, TI * TJ), BF),
            pltpu.VMEM((CC, CZ), F32),
            pltpu.VMEM((TI * TJ, CZ), BF),
            pltpu.VMEM((TI * TJ, CZ), BF),
            pltpu.VMEM((S, C * TJ), BF),
            pltpu.SemaphoreType.DMA((3,)),
        ],
        compiler_params=pltpu.CompilerParams(vmem_limit_bytes=40 << 20),
        cost_estimate=COST,
        name="forward",
    )(*args)


def backward_call(*args):
    return pl.pallas_call(
        backward_kernel,
        in_specs=[SCALARS, FAR, FAR, WHOLE, WHOLE],
        out_specs=(WHOLE,) * 3,
        out_shape=(
            jax.ShapeDtypeStruct((4, 4, 4, C * TJ), F32),
            jax.ShapeDtypeStruct((4, 4, 4, C * TJ), BF),
            jax.ShapeDtypeStruct((S, TI * C), BF),
        ),
        scratch_shapes=[
            pltpu.VMEM((TI * C, C * TJ), BF),
            pltpu.VMEM((TI * TJ, CZ), BF),
            pltpu.VMEM((S, C * TJ), BF),
            pltpu.SemaphoreType.DMA((2,)),
        ],
        compiler_params=pltpu.CompilerParams(vmem_limit_bytes=40 << 20),
        cost_estimate=COST,
        name="backward",
    )(*args)


def shift(x, axis, k):
    return lax.ppermute(x, axis, [(i, (i + k) % 4) for i in range(4)])


def gather4(x, axis):
    return jnp.stack([x] + [shift(x, axis, k) for k in (1, 2, 3)])


def reduce4(x, axis):
    return x[0].astype(F32) + sum(shift(x[k], axis, k).astype(F32) for k in (1, 2, 3))


def swap(x):
    return lax.ppermute(x, "c", [(0, 1), (1, 0)])


def exchange(x, axes):
    return lax.all_to_all(x, axes, split_axis=0, concat_axis=0, tiled=True)


def spread(x, axes, n):
    return exchange(jnp.broadcast_to(x[None], (n,) + x.shape), axes)


def on_device(left_act, right_act, out_weight, out_bias, pair_grad):
    pos = jnp.stack([lax.axis_index("h"), lax.axis_index("x"), lax.axis_index("c")])
    mine = gather4(gather4(right_act.T.reshape(4, C * TJ), "h"), "x")
    left = (left_act * (1.0 / S)).astype(BF).reshape(TI, 16, C).transpose(1, 0, 2)
    a = spread(left.reshape(16, TI * C), COL, 8).reshape(S, TI * C)
    mine, a = lax.optimization_barrier((mine, a))
    other = swap(mine)
    w = out_weight.reshape(C, C, CZ).transpose(1, 0, 2).reshape(CC, CZ)
    pair_out, dp, b, wg = forward_call(
        pos, a, mine, other, w.T, out_bias.reshape(1, CZ), pair_grad.reshape(TI * TJ, CZ)
    )
    wg = exchange(wg, ROW)
    r_own, r_oth, l = backward_call(pos, dp, b, w, a)
    moved = [swap(r_oth[k]) for k in range(4)]
    wg, l, _ = lax.optimization_barrier((wg, l, moved))
    wg = jnp.sum(wg.astype(F32), axis=0).reshape(5, TI * C)
    high = lax.reduce_precision(wg, 8, 7)
    pair = jnp.concatenate([high, wg - high, jnp.zeros((6, TI * C), F32)], axis=0).astype(BF)
    both = exchange(
        jnp.concatenate(
            [l.reshape(8, 16, TI * C), jnp.broadcast_to(pair[None], (8, 16, TI * C))], axis=1
        ),
        COL,
    )
    both = jnp.sum(both.astype(F32), axis=0)
    left_grad = both[:16].reshape(16, TI, C).transpose(1, 0, 2).reshape(TI, 16 * C)
    wg = (both[16:21] + both[21:26]).reshape(C + 8, CZ) * (1.0 / (TI * 32))
    bias_grad = wg[C]
    full = spread(wg[:C].astype(BF), ROW, 32)
    full, left_grad, bias_grad = lax.optimization_barrier((full, left_grad, bias_grad))
    weight_grad = full.astype(F32).reshape(CC, CZ)
    r = [(r_own[k] + moved[k].astype(F32)).astype(BF) for k in range(4)]
    right_sum = reduce4(reduce4(r, "x"), "h")
    right_grad = right_sum.reshape(4 * C, TJ).T
    return (
        pair_out.reshape(TI, TJ, CZ),
        left_grad,
        right_grad,
        weight_grad,
        bias_grad,
    )


def solution(mesh):
    fine = Mesh(mesh.devices.reshape(4, 4, 2, 2, 4), AXES)
    in_specs = (P(ROW, COL), P(COL, ROW), P(), P(), P(ROW, COL, None))
    out_specs = (P(ROW, COL, None), P(ROW, COL), P(COL, ROW), P(), P())
    return jax.shard_map(
        on_device, mesh=fine, in_specs=in_specs, out_specs=out_specs, check_vma=False
    )
```

```python
import jax
import jax.numpy as jnp
from jax import lax
from jax.experimental import pallas as pl
from jax.experimental.pallas import tpu as pltpu
from jax.sharding import Mesh, PartitionSpec as P

S = 128
C = 32
CZ = 128
CC = C * C
TI = 32
TJ = 128
BF = jnp.bfloat16
F32 = jnp.float32
AXES = ("h", "x", "c", "l", "y")
ROW = ("h", "x", "c")
CHIP = ("h", "x")
COL = ("l", "y")
COST = pl.CostEstimate(flops=6 << 30, transcendentals=0, bytes_accessed=4 << 20)
NN = (((1,), (0,)), ((), ()))
NT = (((1,), (1,)), ((), ()))


def forward_kernel(
    pos_ref, a_ref, mine_ref, other_ref, wt_ref, bias_ref, g_ref,
    po_out, dp_out, b_out, wg_ref,
    at, rows, x, wsum, po_ref, dp_ref, b_ref, sems,
):
    first = pos_ref[2] == 0
    for k in range(4):
        for m in range(4):
            t = ((pos_ref[0] + 4 - m) % 4) * 4 + (pos_ref[1] + 4 - k) % 4
            u = mine_ref[k, m].astype(F32)
            v = other_ref[k, m].astype(F32)
            rows[pl.ds(pl.multiple_of(t * 8, 8), 8), :] = jnp.concatenate(
                [jnp.where(first, u, v), jnp.where(first, v, u)], axis=0
            )
    b_ref[...] = rows[...].astype(BF)
    b_copy = pltpu.make_async_copy(b_ref, b_out.at[pl.ds(0, S)], sems.at[0])
    b_copy.start()
    at[...] = a_ref[...].astype(F32).T.astype(BF)
    for n in range(C // 2):
        o = lax.dot_general(
            at[...], b_ref[:, n * 256 : (n + 1) * 256], NN, preferred_element_type=F32
        ).astype(BF)
        for e in range(2):
            d = 2 * n + e
            for i in range(TI):
                x[d * C : (d + 1) * C, i * TJ : (i + 1) * TJ] = o[
                    i * C : (i + 1) * C, e * TJ : (e + 1) * TJ
                ]
    bias = bias_ref[0:1, :]
    total = jnp.zeros((8, CZ), F32)
    for q in range(8):
        pre_t = lax.dot_general(
            wt_ref[...], x[:, q * 512 : (q + 1) * 512], NN, preferred_element_type=F32
        )
        pre = pre_t.T + bias
        sig = 1.0 / (1.0 + jnp.exp(-pre))
        po_ref[q * 512 : (q + 1) * 512, :] = (pre * sig).astype(BF)
        slope = sig * (1.0 + pre * (1.0 - sig))
        dpre = (g_ref[q * 512 : (q + 1) * 512, :].astype(F32) * slope).astype(BF)
        dp_ref[q * 512 : (q + 1) * 512, :] = dpre
        total = total + jnp.sum(dpre.astype(F32).reshape(64, 8, CZ), axis=0)
    dp_copy = pltpu.make_async_copy(dp_ref, dp_out.at[pl.ds(0, TI * TJ)], sems.at[1])
    dp_copy.start()
    po_copy = pltpu.make_async_copy(po_ref, po_out, sems.at[2])
    po_copy.start()
    for m in range(4):
        w = lax.dot_general(
            x[m * 256 : (m + 1) * 256, :], dp_ref[...], NN, preferred_element_type=F32
        )
        for k in range(8):
            wsum[pl.ds(m * 8 + k, C, stride=C), :] = w[k * C : (k + 1) * C, :]
    row = jnp.broadcast_to(jnp.sum(total, axis=0, keepdims=True), (8, CZ))
    for c in range(C):
        wg_ref[c, :, :] = jnp.concatenate([wsum[c * C : (c + 1) * C, :], row], axis=0).astype(BF)
    b_copy.wait()
    dp_copy.wait()
    po_copy.wait()


def backward_kernel(
    pos_ref, dp_in, b_in, w_ref, a_ref, rm_ref, ro_ref, l_ref, dd, dp_ref, b_ref, sems
):
    first = pos_ref[2] == 0
    dp_copies = [
        pltpu.make_async_copy(
            dp_in.at[pl.ds(1024 * n, 1024)], dp_ref.at[pl.ds(1024 * n, 1024)], sems.at[1 + n]
        )
        for n in range(4)
    ]
    for copy in dp_copies:
        copy.start()
    b_copy = pltpu.make_async_copy(b_in.at[pl.ds(0, S)], b_ref, sems.at[0])
    b_copy.start()
    for q in range(TI // 2):
        if q % 4 == 0:
            dp_copies[q // 4].wait()
        g = lax.dot_general(
            w_ref[...], dp_ref[q * 256 : (q + 1) * 256, :], NT, preferred_element_type=F32
        ).astype(BF)
        for e in range(2):
            i = 2 * q + e
            for d in range(C):
                dd[i * C : (i + 1) * C, d * TJ : (d + 1) * TJ] = g[
                    d * C : (d + 1) * C, e * TJ : (e + 1) * TJ
                ]
    for n in range(8):
        r = lax.dot_general(
            a_ref[...], dd[:, n * 512 : (n + 1) * 512], NN, preferred_element_type=F32
        )
        for t in range(16):
            k = (t % 4 + 4 - pos_ref[1]) % 4
            m = (t // 4 + 4 - pos_ref[0]) % 4
            u = r[8 * t : 8 * t + 4, :]
            v = r[8 * t + 4 : 8 * t + 8, :]
            rm_ref[k, m, :, n * 512 : (n + 1) * 512] = jnp.where(first, u, v)
            ro_ref[k, m, :, n * 512 : (n + 1) * 512] = jnp.where(first, v, u).astype(BF)
    b_copy.wait()
    for m in range(4):
        t = lax.dot_general(
            dd[m * 256 : (m + 1) * 256, :], b_ref[...], NT, preferred_element_type=F32
        )
        l_ref[:, m * 256 : (m + 1) * 256] = (t.T * (1.0 / S)).astype(BF)


SCALARS = pl.BlockSpec(memory_space=pltpu.SMEM)
FAR = pl.BlockSpec(memory_space=pltpu.HBM)
WHOLE = pl.BlockSpec(memory_space=pltpu.VMEM)


def forward_call(*args):
    return pl.pallas_call(
        forward_kernel,
        in_specs=[SCALARS] + [WHOLE] * 6,
        out_specs=(FAR, FAR, FAR, WHOLE),
        out_shape=(
            jax.ShapeDtypeStruct((TI * TJ, CZ), BF),
            jax.ShapeDtypeStruct((30 * TI * TJ, CZ), BF),
            jax.ShapeDtypeStruct((30 * S, C * TJ), BF),
            jax.ShapeDtypeStruct((C, C + 8, CZ), BF),
        ),
        scratch_shapes=[
            pltpu.VMEM((TI * C, S), BF),
            pltpu.VMEM((S, C * TJ), F32),
            pltpu.VMEM((CC, TI * TJ), BF),
            pltpu.VMEM((CC, CZ), F32),
            pltpu.VMEM((TI * TJ, CZ), BF),
            pltpu.VMEM((TI * TJ, CZ), BF),
            pltpu.VMEM((S, C * TJ), BF),
            pltpu.SemaphoreType.DMA((3,)),
        ],
        compiler_params=pltpu.CompilerParams(vmem_limit_bytes=40 << 20),
        cost_estimate=COST,
        name="forward",
    )(*args)


def backward_call(*args):
    return pl.pallas_call(
        backward_kernel,
        in_specs=[SCALARS, FAR, FAR, WHOLE, WHOLE],
        out_specs=(WHOLE,) * 3,
        out_shape=(
            jax.ShapeDtypeStruct((4, 4, 4, C * TJ), F32),
            jax.ShapeDtypeStruct((4, 4, 4, C * TJ), BF),
            jax.ShapeDtypeStruct((S, TI * C), BF),
        ),
        scratch_shapes=[
            pltpu.VMEM((TI * C, C * TJ), BF),
            pltpu.VMEM((TI * TJ, CZ), BF),
            pltpu.VMEM((S, C * TJ), BF),
            pltpu.SemaphoreType.DMA((5,)),
        ],
        compiler_params=pltpu.CompilerParams(vmem_limit_bytes=40 << 20),
        cost_estimate=COST,
        name="backward",
    )(*args)


def shift(x, axis, k):
    return lax.ppermute(x, axis, [(i, (i + k) % 4) for i in range(4)])


def gather4(x, axis):
    return jnp.stack([x] + [shift(x, axis, k) for k in (1, 2, 3)])


def reduce4(x, axis):
    return x[0].astype(F32) + sum(shift(x[k], axis, k).astype(F32) for k in (1, 2, 3))


def swap(x):
    return lax.ppermute(x, "c", [(0, 1), (1, 0)])


def exchange(x, axes):
    return lax.all_to_all(x, axes, split_axis=0, concat_axis=0, tiled=True)


def spread(x, axes, n):
    return exchange(jnp.broadcast_to(x[None], (n,) + x.shape), axes)


def on_device(left_act, right_act, out_weight, out_bias, pair_grad):
    pos = jnp.stack([lax.axis_index("h"), lax.axis_index("x"), lax.axis_index("c")])
    mine = gather4(gather4(right_act.T.reshape(4, C * TJ), "h"), "x")
    left = (left_act * (1.0 / S)).astype(BF).reshape(TI, 16, C).transpose(1, 0, 2)
    a = spread(left.reshape(16, TI * C), COL, 8).reshape(S, TI * C)
    bias = jnp.broadcast_to(out_bias, (8, CZ))
    mine, a, bias = lax.optimization_barrier((mine, a, bias))
    other = swap(mine)
    w = out_weight.reshape(C, C, CZ).transpose(1, 0, 2).reshape(CC, CZ)
    pair_out, dp, b, wg = forward_call(
        pos, a, mine, other, w.T, bias, pair_grad.reshape(TI * TJ, CZ)
    )
    wg = exchange(wg, ROW)
    r_own, r_oth, l = backward_call(pos, dp, b, w, a)
    moved = [swap(r_oth[k]) for k in range(4)]
    wg, l, r_own, moved = lax.optimization_barrier((wg, l, r_own, moved))
    wg = jnp.sum(wg.astype(F32), axis=0).reshape(5, TI * C)
    high = lax.reduce_precision(wg, 8, 7)
    pair = jnp.concatenate([high, wg - high, jnp.zeros((6, TI * C), F32)], axis=0).astype(BF)
    both = exchange(
        jnp.concatenate(
            [l.reshape(8, 16, TI * C), jnp.broadcast_to(pair[None], (8, 16, TI * C))], axis=1
        ),
        COL,
    )
    both = jnp.sum(both.astype(F32), axis=0)
    left_grad = both[:16].reshape(16, TI, C).transpose(1, 0, 2).reshape(TI, 16 * C)
    wg = (both[16:21] + both[21:26]).reshape(C + 8, CZ) * (1.0 / (TI * 32))
    bias_grad = wg[C]
    full = spread(wg[:C].astype(BF), ROW, 32)
    full, left_grad, bias_grad = lax.optimization_barrier((full, left_grad, bias_grad))
    weight_grad = full.astype(F32).reshape(CC, CZ)
    r = [(r_own[k] + moved[k].astype(F32)).astype(BF) for k in range(4)]
    right_sum = reduce4(reduce4(r, "x"), "h")
    right_grad = right_sum.reshape(4 * C, TJ).T
    return (
        pair_out.reshape(TI, TJ, CZ),
        left_grad,
        right_grad,
        weight_grad,
        bias_grad,
    )


def solution(mesh):
    fine = Mesh(mesh.devices.reshape(4, 4, 2, 2, 4), AXES)
    in_specs = (P(ROW, COL), P(COL, ROW), P(), P(), P(ROW, COL, None))
    out_specs = (P(ROW, COL, None), P(ROW, COL), P(COL, ROW), P(), P())
    return jax.shard_map(
        on_device, mesh=fine, in_specs=in_specs, out_specs=out_specs, check_vma=False
    )
```

```python
import jax
import jax.numpy as jnp
from jax import lax
from jax.experimental import pallas as pl
from jax.experimental.pallas import tpu as pltpu
from jax.sharding import Mesh, PartitionSpec as P

S = 128
C = 32
CZ = 128
CC = C * C
TI = 32
TJ = 128
BF = jnp.bfloat16
F32 = jnp.float32
AXES = ("h", "x", "c", "l", "y")
ROW = ("h", "x", "c")
CHIP = ("h", "x")
COL = ("l", "y")
COST = pl.CostEstimate(flops=6 << 30, transcendentals=0, bytes_accessed=4 << 20)
NN = (((1,), (0,)), ((), ()))
NT = (((1,), (1,)), ((), ()))


def forward_kernel(
    pos_ref, a_ref, mine_ref, other_ref, wt_ref, bias_ref, g_ref,
    po_out, dp_out, b_out, wg_ref,
    at, rows, x, wsum, po_ref, dp_ref, b_ref, sems,
):
    first = pos_ref[2] == 0
    for k in range(4):
        for m in range(4):
            t = ((pos_ref[0] + 4 - m) % 4) * 4 + (pos_ref[1] + 4 - k) % 4
            u = mine_ref[k, m].astype(F32)
            v = other_ref[k, m].astype(F32)
            rows[pl.ds(pl.multiple_of(t * 8, 8), 8), :] = jnp.concatenate(
                [jnp.where(first, u, v), jnp.where(first, v, u)], axis=0
            )
    b_ref[...] = rows[...].astype(BF)
    b_copy = pltpu.make_async_copy(b_ref, b_out.at[pl.ds(0, S)], sems.at[0])
    b_copy.start()
    at[...] = a_ref[...].astype(F32).T.astype(BF)
    for n in range(C // 2):
        o = lax.dot_general(
            at[...], b_ref[:, n * 256 : (n + 1) * 256], NN, preferred_element_type=F32
        ).astype(BF)
        for e in range(2):
            d = 2 * n + e
            for i in range(TI):
                x[d * C : (d + 1) * C, i * TJ : (i + 1) * TJ] = o[
                    i * C : (i + 1) * C, e * TJ : (e + 1) * TJ
                ]
    bias = bias_ref[0:1, :]
    total = jnp.zeros((8, CZ), F32)
    for q in range(8):
        pre_t = lax.dot_general(
            wt_ref[...], x[:, q * 512 : (q + 1) * 512], NN, preferred_element_type=F32
        )
        pre = pre_t.T + bias
        sig = 1.0 / (1.0 + jnp.exp(-pre))
        po_ref[q * 512 : (q + 1) * 512, :] = (pre * sig).astype(BF)
        slope = sig * (1.0 + pre * (1.0 - sig))
        dpre = (g_ref[q * 512 : (q + 1) * 512, :].astype(F32) * slope).astype(BF)
        dp_ref[q * 512 : (q + 1) * 512, :] = dpre
        total = total + jnp.sum(dpre.astype(F32).reshape(64, 8, CZ), axis=0)
    dp_copy = pltpu.make_async_copy(dp_ref, dp_out.at[pl.ds(0, TI * TJ)], sems.at[1])
    dp_copy.start()
    po_copy = pltpu.make_async_copy(po_ref, po_out, sems.at[2])
    po_copy.start()
    for m in range(4):
        w = lax.dot_general(
            x[m * 256 : (m + 1) * 256, :], dp_ref[...], NN, preferred_element_type=F32
        )
        for k in range(8):
            wsum[pl.ds(m * 8 + k, C, stride=C), :] = w[k * C : (k + 1) * C, :]
    row = jnp.broadcast_to(jnp.sum(total, axis=0, keepdims=True), (8, CZ))
    for c in range(C):
        wg_ref[c, :, :] = jnp.concatenate([wsum[c * C : (c + 1) * C, :], row], axis=0).astype(BF)
    b_copy.wait()
    dp_copy.wait()
    po_copy.wait()


def backward_kernel(
    pos_ref, dp_in, b_in, w_ref, a_ref, rm_ref, ro_ref, l_ref, dd, dp_ref, b_ref, sems
):
    first = pos_ref[2] == 0
    dp_copies = [
        pltpu.make_async_copy(
            dp_in.at[pl.ds(1024 * n, 1024)], dp_ref.at[pl.ds(1024 * n, 1024)], sems.at[1 + n]
        )
        for n in range(4)
    ]
    for copy in dp_copies:
        copy.start()
    b_copy = pltpu.make_async_copy(b_in.at[pl.ds(0, S)], b_ref, sems.at[0])
    b_copy.start()
    for q in range(TI // 2):
        if q % 4 == 0:
            dp_copies[q // 4].wait()
        g = lax.dot_general(
            w_ref[...], dp_ref[q * 256 : (q + 1) * 256, :], NT, preferred_element_type=F32
        ).astype(BF)
        for e in range(2):
            i = 2 * q + e
            for d in range(C):
                dd[i * C : (i + 1) * C, d * TJ : (d + 1) * TJ] = g[
                    d * C : (d + 1) * C, e * TJ : (e + 1) * TJ
                ]
    for n in range(8):
        r = lax.dot_general(
            a_ref[...], dd[:, n * 512 : (n + 1) * 512], NN, preferred_element_type=F32
        )
        for t in range(16):
            k = (t % 4 + 4 - pos_ref[1]) % 4
            m = (t // 4 + 4 - pos_ref[0]) % 4
            u = r[8 * t : 8 * t + 4, :]
            v = r[8 * t + 4 : 8 * t + 8, :]
            rm_ref[k, m, :, n * 512 : (n + 1) * 512] = jnp.where(first, u, v)
            ro_ref[k, m, :, n * 512 : (n + 1) * 512] = jnp.where(first, v, u).astype(BF)
    b_copy.wait()
    for m in range(4):
        t = lax.dot_general(
            dd[m * 256 : (m + 1) * 256, :], b_ref[...], NT, preferred_element_type=F32
        )
        l_ref[:, m * 256 : (m + 1) * 256] = (t.T * (1.0 / S)).astype(BF)


SCALARS = pl.BlockSpec(memory_space=pltpu.SMEM)
FAR = pl.BlockSpec(memory_space=pltpu.HBM)
WHOLE = pl.BlockSpec(memory_space=pltpu.VMEM)


def forward_call(*args):
    return pl.pallas_call(
        forward_kernel,
        in_specs=[SCALARS] + [WHOLE] * 6,
        out_specs=(FAR, FAR, FAR, WHOLE),
        out_shape=(
            jax.ShapeDtypeStruct((TI * TJ, CZ), BF),
            jax.ShapeDtypeStruct((30 * TI * TJ, CZ), BF),
            jax.ShapeDtypeStruct((30 * S, C * TJ), BF),
            jax.ShapeDtypeStruct((C, C + 8, CZ), BF),
        ),
        scratch_shapes=[
            pltpu.VMEM((TI * C, S), BF),
            pltpu.VMEM((S, C * TJ), F32),
            pltpu.VMEM((CC, TI * TJ), BF),
            pltpu.VMEM((CC, CZ), F32),
            pltpu.VMEM((TI * TJ, CZ), BF),
            pltpu.VMEM((TI * TJ, CZ), BF),
            pltpu.VMEM((S, C * TJ), BF),
            pltpu.SemaphoreType.DMA((3,)),
        ],
        compiler_params=pltpu.CompilerParams(vmem_limit_bytes=40 << 20),
        cost_estimate=COST,
        name="forward",
    )(*args)


def backward_call(*args):
    return pl.pallas_call(
        backward_kernel,
        in_specs=[SCALARS, FAR, FAR, WHOLE, WHOLE],
        out_specs=(WHOLE,) * 3,
        out_shape=(
            jax.ShapeDtypeStruct((4, 4, 4, C * TJ), F32),
            jax.ShapeDtypeStruct((4, 4, 4, C * TJ), BF),
            jax.ShapeDtypeStruct((S, TI * C), BF),
        ),
        scratch_shapes=[
            pltpu.VMEM((TI * C, C * TJ), BF),
            pltpu.VMEM((TI * TJ, CZ), BF),
            pltpu.VMEM((S, C * TJ), BF),
            pltpu.SemaphoreType.DMA((5,)),
        ],
        compiler_params=pltpu.CompilerParams(vmem_limit_bytes=40 << 20),
        cost_estimate=COST,
        name="backward",
    )(*args)


def shift(x, axis, k):
    return lax.ppermute(x, axis, [(i, (i + k) % 4) for i in range(4)])


def gather4(x, axis):
    return jnp.stack([x] + [shift(x, axis, k) for k in (1, 2, 3)])


def reduce4(x, axis):
    return x[0].astype(F32) + sum(shift(x[k], axis, k).astype(F32) for k in (1, 2, 3))


def swap(x):
    return lax.ppermute(x, "c", [(0, 1), (1, 0)])


def exchange(x, axes):
    return lax.all_to_all(x, axes, split_axis=0, concat_axis=0, tiled=True)


def spread(x, axes, n):
    return exchange(jnp.broadcast_to(x[None], (n,) + x.shape), axes)


def on_device(left_act, right_act, out_weight, out_bias, pair_grad):
    pos = jnp.stack([lax.axis_index("h"), lax.axis_index("x"), lax.axis_index("c")])
    mine = gather4(gather4(right_act.T.reshape(4, C * TJ), "h"), "x")
    left = (left_act * (1.0 / S)).astype(BF).reshape(TI, 16, C).transpose(1, 0, 2)
    a = spread(left.reshape(16, TI * C), COL, 8).reshape(S, TI * C)
    bias = jnp.broadcast_to(out_bias, (8, CZ))
    mine, a, bias = lax.optimization_barrier((mine, a, bias))
    other = swap(mine)
    w = out_weight.reshape(C, C, CZ).transpose(1, 0, 2).reshape(CC, CZ)
    pair_out, dp, b, wg = forward_call(
        pos, a, mine, other, w.T, bias, pair_grad.reshape(TI * TJ, CZ)
    )
    wg = exchange(wg, ROW)
    r_own, r_oth, l = backward_call(pos, dp, b, w, a)
    moved = [swap(r_oth[k]) for k in range(4)]
    wg, l, r_own, moved = lax.optimization_barrier((wg, l, r_own, moved))
    wg = jnp.sum(wg.astype(F32), axis=0).reshape(5, TI * C)
    both = exchange(
        jnp.concatenate(
            [
                l.reshape(8, 16, TI * C),
                jnp.broadcast_to(jnp.pad(wg.astype(BF), ((0, 3), (0, 0)))[None], (8, 8, TI * C)),
            ],
            axis=1,
        ),
        COL,
    )
    both = jnp.sum(both.astype(F32), axis=0)
    left_grad = both[:16].reshape(16, TI, C).transpose(1, 0, 2).reshape(TI, 16 * C)
    wg = both[16:21].reshape(C + 8, CZ) * (1.0 / (TI * 32))
    bias_grad = wg[C]
    full = spread(wg[:C].astype(BF), ROW, 32)
    full, left_grad, bias_grad = lax.optimization_barrier((full, left_grad, bias_grad))
    weight_grad = full.astype(F32).reshape(CC, CZ)
    r = [(r_own[k] + moved[k].astype(F32)).astype(BF) for k in range(4)]
    right_sum = reduce4(reduce4(r, "x"), "h")
    right_grad = right_sum.reshape(4 * C, TJ).T
    return (
        pair_out.reshape(TI, TJ, CZ),
        left_grad,
        right_grad,
        weight_grad,
        bias_grad,
    )


def solution(mesh):
    fine = Mesh(mesh.devices.reshape(4, 4, 2, 2, 4), AXES)
    in_specs = (P(ROW, COL), P(COL, ROW), P(), P(), P(ROW, COL, None))
    out_specs = (P(ROW, COL, None), P(ROW, COL), P(COL, ROW), P(), P())
    return jax.shard_map(
        on_device, mesh=fine, in_specs=in_specs, out_specs=out_specs, check_vma=False
    )
```

```python
import jax
import jax.numpy as jnp
from jax import lax
from jax.experimental import pallas as pl
from jax.experimental.pallas import tpu as pltpu
from jax.sharding import Mesh, PartitionSpec as P

S = 128
C = 32
CZ = 128
CC = C * C
TI = 32
TJ = 128
BF = jnp.bfloat16
F32 = jnp.float32
AXES = ("h", "x", "c", "l", "y")
ROW = ("h", "x", "c")
CHIP = ("h", "x")
COL = ("l", "y")
COST = pl.CostEstimate(flops=6 << 30, transcendentals=0, bytes_accessed=4 << 20)
NN = (((1,), (0,)), ((), ()))
NT = (((1,), (1,)), ((), ()))


def forward_kernel(
    pos_ref, a_ref, mine_ref, other_ref, wt_ref, bias_ref, g_ref,
    po_out, dp_out, b_out, wg_ref,
    at, rows, x, wsum, po_ref, dp_ref, b_ref, sems,
):
    first = pos_ref[2] == 0
    for k in range(4):
        for m in range(4):
            t = ((pos_ref[0] + 4 - m) % 4) * 4 + (pos_ref[1] + 4 - k) % 4
            u = mine_ref[k, m].astype(F32)
            v = other_ref[k, m].astype(F32)
            rows[pl.ds(pl.multiple_of(t * 8, 8), 8), :] = jnp.concatenate(
                [jnp.where(first, u, v), jnp.where(first, v, u)], axis=0
            )
    b_ref[...] = rows[...].astype(BF)
    b_copy = pltpu.make_async_copy(b_ref, b_out, sems.at[0])
    b_copy.start()
    at[...] = a_ref[...].astype(F32).T.astype(BF)
    for n in range(C // 2):
        o = lax.dot_general(
            at[...], b_ref[:, n * 256 : (n + 1) * 256], NN, preferred_element_type=F32
        ).astype(BF)
        for e in range(2):
            d = 2 * n + e
            for i in range(TI):
                x[d * C : (d + 1) * C, i * TJ : (i + 1) * TJ] = o[
                    i * C : (i + 1) * C, e * TJ : (e + 1) * TJ
                ]
    bias = bias_ref[...]
    total = jnp.zeros((8, CZ), F32)
    for q in range(8):
        pre_t = lax.dot_general(
            wt_ref[...], x[:, q * 512 : (q + 1) * 512], NN, preferred_element_type=F32
        )
        pre = pre_t.T + bias
        sig = 1.0 / (1.0 + jnp.exp(-pre))
        po_ref[q * 512 : (q + 1) * 512, :] = (pre * sig).astype(BF)
        slope = sig * (1.0 + pre * (1.0 - sig))
        dpre = (g_ref[q * 512 : (q + 1) * 512, :].astype(F32) * slope).astype(BF)
        dp_ref[q * 512 : (q + 1) * 512, :] = dpre
        total = total + jnp.sum(dpre.astype(F32).reshape(64, 8, CZ), axis=0)
    dp_copy = pltpu.make_async_copy(dp_ref, dp_out, sems.at[1])
    dp_copy.start()
    po_copy = pltpu.make_async_copy(po_ref, po_out, sems.at[2])
    po_copy.start()
    for m in range(4):
        w = lax.dot_general(
            x[m * 256 : (m + 1) * 256, :], dp_ref[...], NN, preferred_element_type=F32
        )
        for k in range(8):
            wsum[pl.ds(m * 8 + k, C, stride=C), :] = w[k * C : (k + 1) * C, :]
    row = jnp.broadcast_to(jnp.sum(total, axis=0, keepdims=True), (8, CZ))
    for c in range(C):
        wg_ref[c, :, :] = jnp.concatenate([wsum[c * C : (c + 1) * C, :], row], axis=0).astype(BF)
    b_copy.wait()
    dp_copy.wait()
    po_copy.wait()


def backward_kernel(
    pos_ref, dp_in, b_in, w_ref, a_ref, rm_ref, ro_ref, l_ref, dd, dp_ref, b_ref, sems
):
    first = pos_ref[2] == 0
    dp_copy = pltpu.make_async_copy(dp_in, dp_ref, sems.at[0])
    dp_copy.start()
    b_copy = pltpu.make_async_copy(b_in, b_ref, sems.at[1])
    b_copy.start()
    dp_copy.wait()
    for q in range(TI // 2):
        g = lax.dot_general(
            w_ref[...], dp_ref[q * 256 : (q + 1) * 256, :], NT, preferred_element_type=F32
        ).astype(BF)
        for e in range(2):
            i = 2 * q + e
            for d in range(C):
                dd[i * C : (i + 1) * C, d * TJ : (d + 1) * TJ] = g[
                    d * C : (d + 1) * C, e * TJ : (e + 1) * TJ
                ]
    for n in range(8):
        r = lax.dot_general(
            a_ref[...], dd[:, n * 512 : (n + 1) * 512], NN, preferred_element_type=F32
        )
        for t in range(16):
            k = (t % 4 + 4 - pos_ref[1]) % 4
            m = (t // 4 + 4 - pos_ref[0]) % 4
            u = r[8 * t : 8 * t + 4, :]
            v = r[8 * t + 4 : 8 * t + 8, :]
            rm_ref[k, m, :, n * 512 : (n + 1) * 512] = jnp.where(first, u, v)
            ro_ref[k, m, :, n * 512 : (n + 1) * 512] = jnp.where(first, v, u).astype(BF)
    b_copy.wait()
    for m in range(4):
        t = lax.dot_general(
            dd[m * 256 : (m + 1) * 256, :], b_ref[...], NT, preferred_element_type=F32
        )
        l_ref[:, m * 256 : (m + 1) * 256] = (t.T * (1.0 / S)).astype(BF)


SCALARS = pl.BlockSpec(memory_space=pltpu.SMEM)
FAR = pl.BlockSpec(memory_space=pltpu.HBM)
WHOLE = pl.BlockSpec(memory_space=pltpu.VMEM)


def forward_call(*args):
    return pl.pallas_call(
        forward_kernel,
        in_specs=[SCALARS] + [WHOLE] * 6,
        out_specs=(FAR, FAR, FAR, WHOLE),
        out_shape=(
            jax.ShapeDtypeStruct((TI * TJ, CZ), BF),
            jax.ShapeDtypeStruct((TI * TJ, CZ), BF),
            jax.ShapeDtypeStruct((S, C * TJ), BF),
            jax.ShapeDtypeStruct((C, C + 8, CZ), BF),
        ),
        scratch_shapes=[
            pltpu.VMEM((TI * C, S), BF),
            pltpu.VMEM((S, C * TJ), F32),
            pltpu.VMEM((CC, TI * TJ), BF),
            pltpu.VMEM((CC, CZ), F32),
            pltpu.VMEM((TI * TJ, CZ), BF),
            pltpu.VMEM((TI * TJ, CZ), BF),
            pltpu.VMEM((S, C * TJ), BF),
            pltpu.SemaphoreType.DMA((3,)),
        ],
        compiler_params=pltpu.CompilerParams(vmem_limit_bytes=40 << 20),
        cost_estimate=COST,
        name="forward",
    )(*args)


def backward_call(*args):
    return pl.pallas_call(
        backward_kernel,
        in_specs=[SCALARS, FAR, FAR, WHOLE, WHOLE],
        out_specs=(WHOLE,) * 3,
        out_shape=(
            jax.ShapeDtypeStruct((4, 4, 4, C * TJ), F32),
            jax.ShapeDtypeStruct((4, 4, 4, C * TJ), BF),
            jax.ShapeDtypeStruct((S, TI * C), BF),
        ),
        scratch_shapes=[
            pltpu.VMEM((TI * C, C * TJ), BF),
            pltpu.VMEM((TI * TJ, CZ), BF),
            pltpu.VMEM((S, C * TJ), BF),
            pltpu.SemaphoreType.DMA((2,)),
        ],
        compiler_params=pltpu.CompilerParams(vmem_limit_bytes=40 << 20),
        cost_estimate=COST,
        name="backward",
    )(*args)


def shift(x, axis, k):
    return lax.ppermute(x, axis, [(i, (i + k) % 4) for i in range(4)])


def gather4(x, axis):
    return jnp.stack([x] + [shift(x, axis, k) for k in (1, 2, 3)])


def reduce4(x, axis):
    return x[0].astype(F32) + sum(shift(x[k], axis, k).astype(F32) for k in (1, 2, 3))


def swap(x):
    return lax.ppermute(x, "c", [(0, 1), (1, 0)])


def exchange(x, axes):
    return lax.all_to_all(x, axes, split_axis=0, concat_axis=0, tiled=True)


def spread(x, axes, n):
    return exchange(jnp.broadcast_to(x[None], (n,) + x.shape), axes)


def on_device(left_act, right_act, out_weight, out_bias, pair_grad):
    pos = jnp.stack([lax.axis_index("h"), lax.axis_index("x"), lax.axis_index("c")])
    mine = gather4(gather4(right_act.T.reshape(4, C * TJ), "h"), "x")
    left = (left_act * (1.0 / S)).astype(BF).reshape(TI, 16, C).transpose(1, 0, 2)
    a = spread(left.reshape(16, TI * C), COL, 8).reshape(S, TI * C)
    mine, a = lax.optimization_barrier((mine, a))
    other = swap(mine)
    w = out_weight.reshape(C, C, CZ).transpose(1, 0, 2).reshape(CC, CZ)
    pair_out, dp, b, wg = forward_call(
        pos, a, mine, other, w.T, out_bias.reshape(1, CZ), pair_grad.reshape(TI * TJ, CZ)
    )
    wg = exchange(wg, ROW)
    r_own, r_oth, l = backward_call(pos, dp, b, w, a)
    moved = [swap(r_oth[k]) for k in range(4)]
    wg, l, _ = lax.optimization_barrier((wg, l, moved))
    wg = jnp.sum(wg.astype(F32), axis=0).reshape(5, TI * C)
    both = exchange(
        jnp.concatenate(
            [
                l.reshape(8, 16, TI * C),
                jnp.broadcast_to(jnp.pad(wg.astype(BF), ((0, 3), (0, 0)))[None], (8, 8, TI * C)),
            ],
            axis=1,
        ),
        COL,
    )
    both = jnp.sum(both.astype(F32), axis=0)
    left_grad = both[:16].reshape(16, TI, C).transpose(1, 0, 2).reshape(TI, 16 * C)
    wg = both[16:21].reshape(C + 8, CZ) * (1.0 / (TI * 32))
    bias_grad = wg[C]
    full = spread(wg[:C].astype(BF), ROW, 32)
    full, left_grad, bias_grad = lax.optimization_barrier((full, left_grad, bias_grad))
    weight_grad = full.astype(F32).reshape(CC, CZ)
    r = [(r_own[k] + moved[k].astype(F32)).astype(BF) for k in range(4)]
    right_sum = reduce4(reduce4(r, "x").astype(BF), "h")
    right_grad = right_sum.reshape(4 * C, TJ).T
    return (
        pair_out.reshape(TI, TJ, CZ),
        left_grad,
        right_grad,
        weight_grad,
        bias_grad,
    )


def solution(mesh):
    fine = Mesh(mesh.devices.reshape(4, 4, 2, 2, 4), AXES)
    in_specs = (P(ROW, COL), P(COL, ROW), P(), P(), P(ROW, COL, None))
    out_specs = (P(ROW, COL, None), P(ROW, COL), P(COL, ROW), P(), P())
    return jax.shard_map(
        on_device, mesh=fine, in_specs=in_specs, out_specs=out_specs, check_vma=False
    )
```
